32 devices in a mesh: row: 4 (over x, core), col: 8 (over z, y).
Axes of the slice: x: 2, y: 2, z: 4, core: 2. Of those that a mesh axis runs over, the one named last changes fastest.
Arguments:
- inputs: bfloat16 [512, 6144], P('col', 'row'), may hold values from -6 to 6
- cotangent: bfloat16 [512, 6144], P('col', 'row'), may hold values from -6 to 6
- weight_in: bfloat16 [6144, 12288], P('row', 'col'), may hold values from -0.078125 to 0.078125
- moment_in: bfloat16 [6144, 12288], P('row', 'col'), may hold values from -5 to 5
- second_in: bfloat16 [6144, 12288], P('row', 'col'), may hold values from 0.049804688 to 2
- weight_out: bfloat16 [12288, 6144], P('col', 'row'), may hold values from -0.0546875 to 0.0546875
- moment_out: bfloat16 [12288, 6144], P('col', 'row'), may hold values from -5 to 5
- second_out: bfloat16 [12288, 6144], P('col', 'row'), may hold values from 0.049804688 to 2
Outputs:
- input_grad: bfloat16 [512, 6144], P('col', 'row')
- update_in: bfloat16 [6144, 12288], P('row', 'col')
- code_moment_in: bfloat16 [6144, 12288], P('row', 'col')
- code_second_in: bfloat16 [6144, 12288], P('row', 'col')
- row_scale_in: float32 [2, 6144], P(None, 'row')
- col_scale_in: float32 [2, 12288], P(None, 'col')
- update_out: bfloat16 [12288, 6144], P('col', 'row')
- code_moment_out: bfloat16 [12288, 6144], P('col', 'row')
- code_second_out: bfloat16 [12288, 6144], P('col', 'row')
- row_scale_out: float32 [2, 12288], P(None, 'col')
- col_scale_out: float32 [2, 6144], P(None, 'row')
The draws below stay inside these ranges and needn't reach their ends.
All inputs are finite; a program needn't handle non-finite values. Where the reference program divides by a largest or mean magnitude, that divisor is 1e-20 or more.
Results may differ from the reference program's by a relative error of at most 0.0049.
Values may be sent and summed in bfloat16 or wider, within the bound.
A program may use at most 192 MiB of HBM per device.

```python
import math
import jax
import jax.numpy as jnp
from jax import lax

D = 6144
FF = 12288
TOKENS = 512


def block_levels(rng, shape, pieces, least, largest):
    loudness, own = 1.0, jax.random.fold_in(rng, 6)
    for axis_at, parts in pieces:
        steps = jnp.exp(jax.random.uniform(jax.random.fold_in(own, axis_at), (parts,), jnp.float32, least / len(pieces), largest / len(pieces)))
        loudness = loudness * jnp.repeat(steps, shape[axis_at] // parts).reshape([-1 if axis == axis_at else 1 for axis in range(len(shape))])
    return loudness


def noise(key, shape, spread, most, split=(), kind=jnp.bfloat16):
    array = spread * jax.random.normal(key, shape, jnp.float32)
    if split:
        array = array * block_levels(key, shape, split, -0.22, 0.18)
    return jnp.clip(array, -most, most).astype(kind)


def setup_inputs(seed: int = 0) -> dict:
    keys = jax.random.split(jax.random.key(seed), 9)
    return {
        "inputs": noise(keys[0], (TOKENS, D), 1.0, 6.0, ((0, 8), (1, 4))),
        "cotangent": noise(keys[1], (TOKENS, D), 1.0, 6.0, ((0, 8), (1, 4))),
        "weight_in": noise(keys[2], (D, FF), D ** -0.5, 0.078125, ((0, 4), (1, 8))),
        "moment_in": noise(keys[3], (D, FF), 1.0, 5.0, ((0, 4), (1, 8))),
        "second_in": jnp.clip(jnp.exp(math.log(2.0) - 3.6927934 * jax.random.uniform(keys[4], (D, FF), jnp.float32) ** block_levels(keys[4], (D, FF), ((0, 4), (1, 8)), -0.2, 0.2)), 0.049804688, 2.0).astype(jnp.bfloat16),
        "weight_out": noise(keys[5], (FF, D), FF ** -0.5, 0.0546875, ((0, 8), (1, 4))),
        "moment_out": noise(keys[6], (FF, D), 1.0, 5.0, ((0, 8), (1, 4))),
        "second_out": jnp.clip(jnp.exp(math.log(2.0) - 3.6927934 * jax.random.uniform(keys[7], (FF, D), jnp.float32) ** block_levels(keys[7], (FF, D), ((0, 8), (1, 4)), -0.2, 0.2)), 0.049804688, 2.0).astype(jnp.bfloat16),
    }


root_half = 0.7071067811865476
normal_density = 0.3989422804014327
momentum_decay = 0.9
second_decay = 0.95
stable_eps = 1e-08
weight_decay = 0.1

def gelu_parts(preact):
    cumulative = 0.5 * (1.0 + lax.erf(preact * root_half))
    density = jnp.exp(-0.5 * preact * preact) * normal_density
    return (preact * cumulative, cumulative + preact * density)

def optimize(weight, moment, second, gradient, factor):
    scaled = gradient * factor
    moment_new = momentum_decay * moment.astype(jnp.float32) + (1.0 - momentum_decay) * scaled
    second_new = second_decay * second.astype(jnp.float32) + (1.0 - second_decay) * scaled * scaled
    update = moment_new / (jnp.sqrt(second_new) + stable_eps) + weight_decay * weight.astype(jnp.float32)
    row_top = jnp.maximum(jnp.stack([lax.optimization_barrier(jnp.max(jnp.abs(moment_new), axis=1)), lax.optimization_barrier(jnp.max(second_new, axis=1))]), 1.0)
    col_top = jnp.maximum(jnp.stack([lax.optimization_barrier(jnp.max(jnp.abs(moment_new), axis=0)), lax.optimization_barrier(jnp.max(second_new, axis=0))]), 1.0)
    code_moment = moment_new / jnp.minimum(row_top[0][:, None], col_top[0][None, :])
    code_second = second_new / jnp.minimum(row_top[1][:, None], col_top[1][None, :])
    return (update.astype(jnp.bfloat16), code_moment.astype(jnp.bfloat16), code_second.astype(jnp.bfloat16), row_top, col_top)

def reference(inputs, cotangent, weight_in, moment_in, second_in, weight_out, moment_out, second_out):
    preact = jnp.dot(inputs, weight_in, preferred_element_type=jnp.float32)
    hidden_grad = jnp.dot(cotangent, weight_out.T, preferred_element_type=jnp.float32)
    activ_value, slope = gelu_parts(preact)
    hidden = activ_value.astype(jnp.bfloat16)
    delta = (hidden_grad * slope).astype(jnp.bfloat16)
    input_grad = jnp.dot(delta, weight_in.T, preferred_element_type=jnp.float32).astype(jnp.bfloat16)
    grad_in = jnp.dot(inputs.T, delta, preferred_element_type=jnp.float32)
    grad_out = jnp.dot(hidden.T, cotangent, preferred_element_type=jnp.float32)
    total = jnp.sum(grad_in * grad_in) + jnp.sum(grad_out * grad_out)
    factor = 1.0 / jnp.maximum(jnp.sqrt(total / (2.0 * D * FF)), 1.0)
    first = optimize(weight_in, moment_in, second_in, grad_in, factor)
    latter = optimize(weight_out, moment_out, second_out, grad_out, factor)
    return (input_grad, first[0], first[1], first[2], first[3], first[4], latter[0], latter[1], latter[2], latter[3], latter[4])
```

```python
import functools

import jax
import jax.numpy as jnp
from jax import lax
from jax.experimental import pallas as pl
from jax.experimental.pallas import tpu as pltpu
from jax.sharding import PartitionSpec as P

root_half = 0.7071067811865476
normal_density = 0.3989422804014327
momentum_decay = 0.9
second_decay = 0.95
stable_eps = 1e-08
weight_decay = 0.1
LANES = 128


def contract(left, right, left_dim, right_dim):
    return lax.dot_general(
        left, right, (((left_dim,), (right_dim,)), ((), ())), preferred_element_type=jnp.float32
    )


def activate(preact, hidden_grad):
    cumulative = 0.5 * (1.0 + lax.erf(preact * root_half))
    density = jnp.exp(-0.5 * preact * preact) * normal_density
    hidden = (preact * cumulative).astype(jnp.bfloat16)
    delta = (hidden_grad * (cumulative + preact * density)).astype(jnp.bfloat16)
    return (hidden, delta)


def exchange_kernel(plan, sizes, *refs):
    count = len(plan)
    sources, targets = refs[:count], refs[count : 2 * count]
    send_sem, recv_sem, own_sem = refs[2 * count :]
    axes = sorted(set(axis for axis, _ in plan))
    me = {axis: lax.axis_index(axis) for axis in axes}
    barrier = pltpu.get_barrier_semaphore()
    greeted = 0
    for axis in axes:
        for step in range(1, sizes[axis]):
            peer = lax.rem(me[axis] + step, sizes[axis])
            pl.semaphore_signal(
                barrier, inc=1, device_id={axis: peer}, device_id_type=pl.DeviceIdType.MESH
            )
            greeted += 1
    owns = []
    for item, (axis, scatter) in enumerate(plan):
        block = sources[item].at[me[axis]] if scatter else sources[item]
        own = pltpu.make_async_copy(block, targets[item].at[me[axis]], own_sem.at[item])
        own.start()
        owns.append(own)
    pl.semaphore_wait(barrier, greeted)
    copies = []
    at = 0
    for item, (axis, scatter) in enumerate(plan):
        for step in range(1, sizes[axis]):
            peer = lax.rem(me[axis] + step, sizes[axis])
            block = sources[item].at[peer] if scatter else sources[item]
            copy = pltpu.make_async_remote_copy(
                src_ref=block,
                dst_ref=targets[item].at[me[axis]],
                send_sem=send_sem.at[at],
                recv_sem=recv_sem.at[at],
                device_id={axis: peer},
                device_id_type=pl.DeviceIdType.MESH,
            )
            copy.start()
            copies.append(copy)
            at += 1
    for own in owns:
        own.wait()
    for copy in copies:
        copy.wait()


def exchange(identity, plan, sizes, *arrays):
    flights = sum(sizes[axis] - 1 for axis, _ in plan)
    shapes = [
        jax.ShapeDtypeStruct(
            array.shape if scatter else (sizes[axis],) + array.shape, array.dtype
        )
        for array, (axis, scatter) in zip(arrays, plan)
    ]
    return pl.pallas_call(
        functools.partial(exchange_kernel, plan, sizes),
        out_shape=shapes,
        in_specs=[pl.BlockSpec(memory_space=pl.ANY)] * len(plan),
        out_specs=[pl.BlockSpec(memory_space=pl.ANY)] * len(plan),
        scratch_shapes=[
            pltpu.SemaphoreType.DMA((flights,)),
            pltpu.SemaphoreType.DMA((flights,)),
            pltpu.SemaphoreType.DMA((len(plan),)),
        ],
        compiler_params=pltpu.CompilerParams(collective_id=identity, has_side_effects=True),
        name=f"exchange{identity}",
    )(*arrays)


def lane_fold(values, combine):
    folded = values[:, :LANES]
    for at in range(LANES, values.shape[1], LANES):
        folded = combine(folded, values[:, at : at + LANES])
    return folded


def squares_kernel(left_ref, right_ref, total_ref):
    gradient = contract(left_ref[...], right_ref[...], 0, 0)
    folded = lane_fold(gradient * gradient, jnp.add)
    folded = jnp.sum(folded.reshape(-1, 8, LANES), axis=0)

    @pl.when(pl.program_id(0) == 0)
    def _():
        total_ref[...] = jnp.zeros_like(total_ref)

    total_ref[...] += folded


def row_block(rows):
    return 256 if rows % 256 == 0 else 128


def squares(left, right):
    tokens, rows = left.shape
    block = row_block(rows)
    return pl.pallas_call(
        squares_kernel,
        grid=(rows // block,),
        out_shape=jax.ShapeDtypeStruct((8, LANES), jnp.float32),
        in_specs=[
            pl.BlockSpec((tokens, block), lambda i: (0, i)),
            pl.BlockSpec(right.shape, lambda i: (0, 0)),
        ],
        out_specs=pl.BlockSpec((8, LANES), lambda i: (0, 0)),
        name="squares",
    )(left, right)


def to_lanes(column_tops):
    pieces = []
    for at in range(0, column_tops.shape[0], LANES):
        turned = column_tops[at : at + LANES].T
        pieces.append(jnp.max(turned, axis=0, keepdims=True))
    return jnp.concatenate(pieces, axis=1)


def moments_kernel(
    factor_ref, left_ref, right_ref, weight_ref, moment_ref, second_ref,
    update_ref, new_moment_ref, new_second_ref, row_ref, col_ref,
):
    gradient = contract(left_ref[...], right_ref[...], 0, 0)
    scaled = gradient * factor_ref[0, 0]
    moment_new = momentum_decay * moment_ref[...].astype(jnp.float32) + (
        1.0 - momentum_decay
    ) * scaled
    second_new = second_decay * second_ref[...].astype(jnp.float32) + (
        1.0 - second_decay
    ) * scaled * scaled
    update = moment_new / (jnp.sqrt(second_new) + stable_eps) + weight_decay * weight_ref[
        ...
    ].astype(jnp.float32)
    update_ref[...] = update.astype(jnp.bfloat16)
    new_moment_ref[...] = moment_new.astype(jnp.bfloat16)
    new_second_ref[...] = second_new.astype(jnp.bfloat16)
    size = jnp.abs(moment_new)
    row_ref[0:1, :] = to_lanes(lane_fold(size, jnp.maximum))
    row_ref[1:2, :] = to_lanes(lane_fold(second_new, jnp.maximum))

    @pl.when(pl.program_id(0) == 0)
    def _():
        col_ref[...] = jnp.zeros_like(col_ref)

    col_ref[0:1, :] = jnp.maximum(col_ref[0:1, :], jnp.max(size, axis=0, keepdims=True))
    col_ref[1:2, :] = jnp.maximum(col_ref[1:2, :], jnp.max(second_new, axis=0, keepdims=True))


def moments(factor, left, right, weight, moment, second):
    rows, cols = weight.shape
    tokens = left.shape[0]
    block = row_block(rows)
    tile = pl.BlockSpec((block, cols), lambda i: (i, 0))
    half = jax.ShapeDtypeStruct((rows, cols), jnp.bfloat16)
    return pl.pallas_call(
        moments_kernel,
        grid=(rows // block,),
        out_shape=[
            half,
            half,
            half,
            jax.ShapeDtypeStruct((2, rows), jnp.float32),
            jax.ShapeDtypeStruct((2, cols), jnp.float32),
        ],
        in_specs=[
            pl.BlockSpec(memory_space=pltpu.SMEM),
            pl.BlockSpec((tokens, block), lambda i: (0, i)),
            pl.BlockSpec((tokens, cols), lambda i: (0, 0)),
            tile,
            tile,
            tile,
        ],
        out_specs=[
            tile,
            tile,
            tile,
            pl.BlockSpec((2, block), lambda i: (0, i)),
            pl.BlockSpec((2, cols), lambda i: (0, 0)),
        ],
        name="moments",
    )(factor, left, right, weight, moment, second)


def encode_kernel(moment_ref, second_ref, row_ref, col_ref, code_moment_ref, code_second_ref):
    rows, cols = moment_ref.shape
    for which, (source, target) in enumerate(
        ((moment_ref, code_moment_ref), (second_ref, code_second_ref))
    ):
        for low in range(0, rows, LANES):
            span = pl.ds(low, LANES)
            inverse = 1.0 / row_ref[which : which + 1, low : low + LANES]
            inverse = jnp.broadcast_to(inverse, (LANES, LANES)).T
            for at in range(0, cols, LANES):
                other = 1.0 / col_ref[which : which + 1, at : at + LANES]
                value = source[span, at : at + LANES].astype(jnp.float32)
                target[span, at : at + LANES] = (value * jnp.maximum(inverse, other)).astype(
                    jnp.bfloat16
                )


def encode(moment, second, row_top, col_top):
    rows, cols = moment.shape
    block = row_block(rows)
    tile = pl.BlockSpec((block, cols), lambda i: (i, 0))
    half = jax.ShapeDtypeStruct((rows, cols), jnp.bfloat16)
    return pl.pallas_call(
        encode_kernel,
        grid=(rows // block,),
        out_shape=[half, half],
        in_specs=[
            tile,
            tile,
            pl.BlockSpec((2, block), lambda i: (0, i)),
            pl.BlockSpec((2, cols), lambda i: (0, 0)),
        ],
        out_specs=[tile, tile],
        name="encode",
    )(moment, second, row_top, col_top)


def shards(
    sizes, inputs, cotangent, weight_in, moment_in, second_in, weight_out, moment_out, second_out
):
    rows, cols = sizes["row"], sizes["col"]
    width_in, hidden_cols = weight_in.shape
    width = inputs.shape[1]
    tokens = inputs.shape[0] * cols
    entries = 2.0 * width_in * rows * hidden_cols * cols
    all_inputs, all_cotangent = exchange(
        0, (("col", False), ("col", False)), sizes, inputs, cotangent
    )
    all_inputs = all_inputs.reshape(tokens, width)
    all_cotangent = all_cotangent.reshape(tokens, width)
    preact_part = contract(all_inputs, weight_in, 1, 0).astype(jnp.bfloat16)
    grad_part = contract(all_cotangent, weight_out, 1, 1).astype(jnp.bfloat16)
    parts = (rows, tokens // rows, hidden_cols)
    preact_parts, grad_parts = exchange(
        1,
        (("row", True), ("row", True)),
        sizes,
        preact_part.reshape(parts),
        grad_part.reshape(parts),
    )
    preact = jnp.sum(preact_parts.astype(jnp.float32), axis=0)
    hidden_grad = jnp.sum(grad_parts.astype(jnp.float32), axis=0)
    hidden, delta = activate(preact, hidden_grad)
    all_hidden, all_delta = exchange(2, (("row", False), ("row", False)), sizes, hidden, delta)
    all_hidden = all_hidden.reshape(tokens, hidden_cols)
    all_delta = all_delta.reshape(tokens, hidden_cols)
    grad_input_part = contract(all_delta, weight_in, 1, 1).astype(jnp.bfloat16)
    local_total = squares(all_inputs, all_delta) + squares(all_hidden, all_cotangent)
    grad_input_parts, totals = exchange(
        3,
        (("col", True), ("col", False)),
        sizes,
        grad_input_part.reshape(cols, tokens // cols, width),
        local_total,
    )
    input_grad = jnp.sum(grad_input_parts.astype(jnp.float32), axis=0).astype(jnp.bfloat16)
    (totals,) = exchange(4, (("row", False),), sizes, jnp.sum(totals, axis=0))
    total = jnp.sum(totals)
    factor = 1.0 / jnp.maximum(jnp.sqrt(total / entries), 1.0)
    factor = factor.reshape(1, 1)
    update_in, moment_new_in, second_new_in, rows_in, cols_in = moments(
        factor, all_inputs, all_delta, weight_in, moment_in, second_in
    )
    update_out, moment_new_out, second_new_out, rows_out, cols_out = moments(
        factor, all_hidden, all_cotangent, weight_out, moment_out, second_out
    )
    rows_in, cols_out, cols_in, rows_out = exchange(
        5,
        (("col", False), ("col", False), ("row", False), ("row", False)),
        sizes,
        rows_in,
        cols_out,
        cols_in,
        rows_out,
    )
    rows_in, cols_out, cols_in, rows_out = (
        jnp.maximum(jnp.max(tops, axis=0), 1.0) for tops in (rows_in, cols_out, cols_in, rows_out)
    )
    code_moment_in, code_second_in = encode(moment_new_in, second_new_in, rows_in, cols_in)
    code_moment_out, code_second_out = encode(moment_new_out, second_new_out, rows_out, cols_out)
    return (
        input_grad,
        update_in,
        code_moment_in,
        code_second_in,
        rows_in,
        cols_in,
        update_out,
        code_moment_out,
        code_second_out,
        rows_out,
        cols_out,
    )


def solution(mesh):
    in_specs = (
        P("col", "row"),
        P("col", "row"),
        P("row", "col"),
        P("row", "col"),
        P("row", "col"),
        P("col", "row"),
        P("col", "row"),
        P("col", "row"),
    )
    out_specs = (
        P("col", "row"),
        P("row", "col"),
        P("row", "col"),
        P("row", "col"),
        P(None, "row"),
        P(None, "col"),
        P("col", "row"),
        P("col", "row"),
        P("col", "row"),
        P(None, "col"),
        P(None, "row"),
    )
    sizes = {axis: mesh.shape[axis] for axis in ("row", "col")}
    return jax.shard_map(
        functools.partial(shards, sizes),
        mesh=mesh,
        in_specs=in_specs,
        out_specs=out_specs,
        check_vma=False,
    )
```
